512 devices in a mesh: row: 32 (over y_hi, z, core), col: 16 (over y_lo, x).
Axes of the slice: x: 4, y: 8 (y_hi: 2, y_lo: 4; y = y_hi * 4 + y_lo), z: 8, core: 2. Of those that a mesh axis runs over, the one named last changes fastest.
Arguments:
- stress: float32 [256, 16384], P('col', 'row'), may hold values from -2.5 to 2.5
- state: float32 [256, 8192], P('col', 'row'), may hold values from 0 to 1
- load_rate: int32 [256, 16384], P('col', 'row'), may hold values from 0 to 2047
- a_param: float32 [8192], P('row'), may hold values from 1 to 2
- b_param: float32 [8192], P('row'), may hold values from 0.25 to 1
- near_band: bfloat16 [16384, 768], P('row'), may hold values from -0.21875 to 0.21875
- u_far: bfloat16 [64, 64, 32, 256], P('row', 'col'), may hold values from -0.1875 to 0.1875
- v_far: bfloat16 [64, 64, 32, 256], P('row', 'col'), may hold values from -0.375 to 0.375
- ranks: int32 [64, 64], P('row', 'col'), may hold values from 1 to 32, as said below
Outputs:
- new_stress: float32 [256, 16384], P('col', 'row')
- new_state: float32 [256, 8192], P('col', 'row')
The draws below stay inside these ranges and needn't reach their ends.
Inputs may be any that keep to these rules, and one draw needn't show every extreme that they name: ranks of blocks with |I - J| <= 1 are not used; blocks with |I - J| = 2 have rank 32.
All inputs are finite; a program needn't handle non-finite values.
Results may differ from the reference program's by a relative error of at most 0.0021.
Values may be sent and summed in bfloat16 or wider, within the bound.
No kernel may reach another device: no remote copies, remote signals or barrier semaphores. Data moves between devices by JAX's collectives and lax.ppermute only.
A program may use at most 64 MiB of HBM per device.

```python
import math
import jax
import jax.numpy as jnp
from jax import lax

B = 128
RK = 32
MEMBERS = 256
NB = 64
NE = 8192
NDOF = 16384


def draw_ranks(key, part):
    drawn = jax.random.randint(key, (NB, NB), 1, RK + 1)
    blocks = jnp.arange(NB)
    spacing = jnp.abs(blocks[:, None] - blocks[None, :])
    return jnp.where(spacing == 2, RK, drawn).astype(jnp.int32)


def set_ends(values, key, least, largest):
    place = [jax.random.randint(jax.random.fold_in(key, axis), (), 0, length) for axis, length in enumerate(values.shape)]
    main_axis = values.shape.index(max(values.shape))
    next_to = place[:main_axis] + [(place[main_axis] + 1) % values.shape[main_axis]] + place[main_axis + 1:]
    return values.at[tuple(place)].set(least).at[tuple(next_to)].set(largest)


def block_levels(stream_key, shape, split, smallest, largest):
    def one(axis_at, shards_of):
        draws = jax.random.uniform(jax.random.fold_in(jax.random.fold_in(stream_key, 6), axis_at), (shards_of,), jnp.float32, smallest / len(split), largest / len(split))
        return jnp.repeat(jnp.exp(draws), shape[axis_at] // shards_of).reshape((-1,) + (1,) * (len(shape) - axis_at - 1))

    factor_of = one(*split[0])
    for cut in split[1:]:
        factor_of = factor_of * one(*cut)
    return factor_of


def normal_values(rng, dims, deviation, bound, cuts=(), kind=jnp.bfloat16):
    result = jax.random.normal(rng, dims, jnp.float32) * deviation
    if len(cuts) > 0:
        result = block_levels(rng, dims, cuts, -0.22, 0.18) * result
    return jnp.clip(result, min=-bound, max=bound).astype(kind)


def setup_inputs(seed: int = 0) -> dict:
    key_of = jax.random.split(jax.random.key(seed), 10)
    stress = normal_values(key_of[0], (MEMBERS, NDOF), 0.3, 2.5, ((0, 16), (1, 32)), jnp.float32)
    state = jnp.clip(1.0 * jax.random.uniform(key_of[1], (MEMBERS, NE), jnp.float32) ** block_levels(key_of[1], (MEMBERS, NE), ((0, 16), (1, 32)), -0.2, 0.2), 0.0, 1.0)
    load_rate = set_ends(jax.random.randint(key_of[2], (MEMBERS, NDOF), 0, 2048), jax.random.fold_in(key_of[2], 1), 0, 2047).astype(jnp.int32)
    a_param = jnp.clip(jnp.exp(math.log(2.0) - 0.6931472 * jax.random.uniform(key_of[3], (NE,), jnp.float32) ** block_levels(key_of[3], (NE,), ((0, 32),), -0.2, 0.2)), 1.0, 2.0)
    b_param = jnp.clip(jnp.exp(math.log(1.0) - 1.3862944 * jax.random.uniform(key_of[4], (NE,), jnp.float32) ** block_levels(key_of[4], (NE,), ((0, 32),), -0.2, 0.2)), 0.25, 1.0)
    near_band = normal_values(key_of[5], (NDOF, 6 * B), (6 * B) ** -0.5, 0.21875, ((0, 32),))
    u_far = normal_values(key_of[6], (NB, NB, RK, 2 * B), (RK * NB // 2) ** -0.5, 0.1875, ((0, 32), (1, 16)))
    v_far = normal_values(key_of[7], (NB, NB, RK, 2 * B), (2 * B) ** -0.5, 0.375, ((0, 32), (1, 16)))
    ranks = draw_ranks(jax.random.fold_in(key_of[9], 71), 0)
    return {"stress": stress, "state": state, "load_rate": load_rate, "a_param": a_param, "b_param": b_param, "near_band": near_band, "u_far": u_far, "v_far": v_far, "ranks": ranks}


HSTEP = 0.2
RATE_UNIT = 1.0 / 1024.0

def rates_and_drift(stress_now, state_now, plate_rate, a_param, b_param):
    members = stress_now.shape[0]
    block_count = a_param.shape[0] // B
    stress_view = stress_now.reshape(members, block_count, 2, B)
    state_view = state_now.reshape(members, block_count, 1, B)
    direct_view = a_param.reshape(1, block_count, 1, B)
    evolve_view = b_param.reshape(1, block_count, B)
    slip_rate = 2.0 * jnp.exp(-state_view) * jnp.sinh(stress_view / direct_view)
    slip_speed = jnp.sqrt(lax.optimization_barrier(jnp.sum(slip_rate * slip_rate, axis=2)))
    drift = evolve_view * (jnp.exp(-state_view[:, :, 0]) - slip_speed)
    excess = (slip_rate - plate_rate.reshape(members, block_count, 2, B)).astype(jnp.bfloat16)
    return (excess.reshape(members, -1), drift.reshape(members, -1))

def reference(stress, state, load_rate, a_param, b_param, near_band, u_far, v_far, ranks):
    plate_rate = load_rate.astype(jnp.float32) * RATE_UNIT
    block_dofs = 2 * B
    slots = jnp.arange(RK, dtype=jnp.int32)
    blocks = jnp.arange(NB, dtype=jnp.int32)

    def tendency(stress_now, state_now):
        excess, drift = rates_and_drift(stress_now, state_now, plate_rate, a_param, b_param)
        grid = excess.reshape(MEMBERS, NB, block_dofs)
        grid_wide = grid.astype(jnp.float32)
        padded = jnp.pad(grid, ((0, 0), (1, 1), (0, 0)))

        def one_row(index):
            v_rows = v_far[index].astype(jnp.float32)
            u_rows = u_far[index].astype(jnp.float32)
            weights = jnp.einsum('mjd,jrd->jmr', grid_wide, v_rows)
            active = (slots[None, :] < ranks[index][:, None]) & (jnp.abs(blocks - index) >= 2)[:, None]
            weights = jnp.where(active[:, None, :], weights, 0.0)
            weights = lax.optimization_barrier(weights.astype(jnp.bfloat16)).astype(jnp.float32)
            distant = jnp.einsum('jmr,jrd->md', weights, u_rows)
            segment = lax.dynamic_slice_in_dim(padded, index, 3, 1).reshape(MEMBERS, 3 * block_dofs)
            local_band = lax.dynamic_slice_in_dim(near_band, index * block_dofs, block_dofs, 0)
            nearby = jnp.dot(segment, local_band.T, preferred_element_type=jnp.float32)
            return distant + nearby
        rows_out = lax.map(one_row, jnp.arange(NB, dtype=jnp.int32))
        totals = jnp.transpose(rows_out, (1, 0, 2)).reshape(MEMBERS, NDOF)
        return (-totals, drift)
    rate_one, drift_one = tendency(stress, state)
    stress_one = stress + HSTEP * rate_one
    state_one = state + HSTEP * drift_one
    rate_two, drift_two = tendency(stress_one, state_one)
    stress_two = 0.75 * stress + 0.25 * (stress_one + HSTEP * rate_two)
    state_two = 0.75 * state + 0.25 * (state_one + HSTEP * drift_two)
    rate_three, drift_three = tendency(stress_two, state_two)
    new_stress = stress / 3.0 + 2.0 / 3.0 * (stress_two + HSTEP * rate_three)
    new_state = state / 3.0 + 2.0 / 3.0 * (state_two + HSTEP * drift_three)
    return (new_stress, new_state)
```

```python
import jax
import jax.numpy as jnp
from jax import lax
from jax.sharding import PartitionSpec as P

B = 128
HSTEP = 0.2
RATE_UNIT = 1.0 / 1024.0


def local(stress, state, load_rate, a_param, b_param, near_band, u_far, v_far, ranks):
    rows = lax.axis_size("row")
    row_index = lax.axis_index("row")
    col_index = lax.axis_index("col")
    block_rows, block_cols, slots, dofs = u_far.shape
    members = stress.shape[0]
    blocks = rows * block_rows

    global_rows = row_index * block_rows + jnp.arange(block_rows, dtype=jnp.int32)
    global_cols = col_index * block_cols + jnp.arange(block_cols, dtype=jnp.int32)
    distant = jnp.abs(global_rows[:, None] - global_cols[None, :]) >= 2
    active = (jnp.arange(slots, dtype=jnp.int32)[None, None, :] < ranks[:, :, None]) & distant[:, :, None]
    v_own = jnp.where(active[..., None], v_far, 0).astype(v_far.dtype)
    v_all = lax.all_gather(jnp.swapaxes(v_own, 0, 1), "col", axis=0, tiled=True)
    u_all = lax.all_gather(jnp.swapaxes(u_far, 0, 1), "col", axis=0, tiled=True)

    def to_blocks(value):
        return jnp.swapaxes(value.reshape(members, block_rows, -1), 0, 1)

    def from_blocks(value):
        return jnp.swapaxes(value, 0, 1).reshape(members, -1)

    plate = to_blocks(load_rate.astype(jnp.float32) * RATE_UNIT)
    stress_start, state_start = to_blocks(stress), to_blocks(state)
    direct = a_param.reshape(block_rows, 1, B)
    evolve = b_param.reshape(block_rows, 1, B)
    band = near_band.reshape(block_rows, dofs, 3, dofs)

    def tendency(stress_now, state_now):
        decay = jnp.exp(-state_now)
        rate_a = 2.0 * decay * jnp.sinh(stress_now[..., :B] / direct)
        rate_b = 2.0 * decay * jnp.sinh(stress_now[..., B:] / direct)
        drift = evolve * (decay - jnp.sqrt(rate_a * rate_a + rate_b * rate_b))
        excess = (jnp.concatenate([rate_a, rate_b], axis=2) - plate).astype(jnp.bfloat16)
        copies = jnp.broadcast_to(excess[None], (rows,) + excess.shape)
        grid = lax.all_to_all(copies, "row", 0, 0).reshape(blocks, members, dofs)
        weights = jnp.einsum("jmd,jird->jmir", grid, v_all, preferred_element_type=jnp.float32)
        weights = weights.astype(jnp.bfloat16)
        total = jnp.einsum("jmir,jird->imd", weights, u_all, preferred_element_type=jnp.float32)
        window = []
        for offset in range(-1, block_rows + 1):
            at = row_index * block_rows + offset
            block = lax.dynamic_index_in_dim(grid, jnp.clip(at, 0, blocks - 1), 0, keepdims=False)
            window.append(jnp.where((at >= 0) & (at < blocks), block, 0).astype(block.dtype))
        windows = jnp.stack([jnp.stack(window[i : i + 3]) for i in range(block_rows)])
        total = total + jnp.einsum("ismd,iksd->imk", windows, band, preferred_element_type=jnp.float32)
        return -total, drift

    rate_one, drift_one = tendency(stress_start, state_start)
    stress_one = stress_start + HSTEP * rate_one
    state_one = state_start + HSTEP * drift_one
    rate_two, drift_two = tendency(stress_one, state_one)
    stress_two = 0.75 * stress_start + 0.25 * (stress_one + HSTEP * rate_two)
    state_two = 0.75 * state_start + 0.25 * (state_one + HSTEP * drift_two)
    rate_three, drift_three = tendency(stress_two, state_two)
    new_stress = stress_start / 3.0 + 2.0 / 3.0 * (stress_two + HSTEP * rate_three)
    new_state = state_start / 3.0 + 2.0 / 3.0 * (state_two + HSTEP * drift_three)
    return from_blocks(new_stress), from_blocks(new_state)


def solution(mesh):
    return jax.shard_map(
        local,
        mesh=mesh,
        in_specs=(
            P("col", "row"),
            P("col", "row"),
            P("col", "row"),
            P("row"),
            P("row"),
            P("row", None),
            P("row", "col", None, None),
            P("row", "col", None, None),
            P("row", "col"),
        ),
        out_specs=(P("col", "row"), P("col", "row")),
        check_vma=False,
    )
```

```python
import functools

import jax
import jax.numpy as jnp
from jax import lax
from jax.experimental import pallas as pl
from jax.experimental.pallas import tpu as pltpu
from jax.sharding import Mesh, PartitionSpec as P

B = 128
HSTEP = 0.2
RATE_UNIT = 1.0 / 1024.0

VMEM = pl.BlockSpec(memory_space=pltpu.VMEM)
SMEM = pl.BlockSpec(memory_space=pltpu.SMEM)
NT = (((1,), (1,)), ((), ()))

YL, X, GROUP, CORE, BIT, ROW, COL = range(7)


def ring(size, step):
    return [(i, (i + step) % size) for i in range(size)]


def split_kernel(place_ref, ranks_ref, v_ref, u_ref, near_ref, keep_ref, send_ref, near_out_ref):
    block_rows, block_cols, slots, dofs = v_ref.shape
    core, bit = place_ref[CORE], place_ref[BIT]
    slot = lax.broadcasted_iota(jnp.int32, (slots, dofs), 0)
    for flip in range(2):
        low = bit if flip == 0 else 1 - bit
        for i in range(block_rows):
            for out_ref, high in ((keep_ref.at[0], core), (send_ref.at[0], 1 - core)):
                j = 2 * high + low
                apart = jnp.abs(place_ref[ROW] * block_rows + i - place_ref[COL] * block_cols - j) >= 2
                rank = jnp.where(apart, ranks_ref[i, j], 0)
                at = (flip * 2 * block_rows + i) * slots
                out_ref[at : at + slots, :] = jnp.where(slot < rank, v_ref[i, j], 0).astype(v_ref.dtype)
                at = at + block_rows * slots
                out_ref[at : at + slots, :] = u_ref[i, j]
    first, second = slice(0, dofs), slice(dofs, 2 * dofs)
    tiles = [slice(s * dofs, (s + 1) * dofs) for s in range(3)]
    near_out_ref[0] = jnp.where(bit == 0, near_ref[first, tiles[1]], near_ref[first, tiles[2]])
    near_out_ref[1] = jnp.where(bit == 0, near_ref[second, tiles[0]], near_ref[second, tiles[1]])
    send_ref[1] = jnp.where(bit == 0, near_ref[second, tiles[2]], near_ref[first, tiles[0]])


def pack_kernel(place_ref, stress_ref, state_ref, load_ref, own_ref, send_ref):
    bit, dofs = place_ref[BIT], 2 * B

    def halves(value):
        low, high = value[:, : value.shape[1] // 2], value[:, value.shape[1] // 2 :]
        return jnp.where(bit == 0, low, high), jnp.where(bit == 0, high, low)

    plate = load_ref[...].astype(jnp.float32) * RATE_UNIT
    for value, at in ((stress_ref[...], 0), (state_ref[...], dofs), (plate, dofs + B)):
        mine, other = halves(value)
        own_ref[:, at : at + mine.shape[1]] = mine
        send_ref[:, at : at + mine.shape[1]] = other


def start_of(own_ref, other_ref):
    both = jnp.concatenate([own_ref[...], other_ref[...]], axis=0)
    return both[:, : 2 * B], both[:, 2 * B : 3 * B], both[:, 3 * B :]


def half_of(place_ref, ref):
    return jnp.where(place_ref[BIT] == 0, ref[:, :B], ref[:, B:])


def rates(stress, state, plate, direct, evolve, copies_ref):
    squares = 0.0
    for s in range(2):
        here = slice(s * B, (s + 1) * B)
        drive = stress[:, here] / direct
        rate = jnp.exp(drive - state) - jnp.exp(-drive - state)
        squares = squares + rate * rate
        excess = (rate - plate[:, here]).astype(jnp.bfloat16)
        for n in range(copies_ref.shape[0]):
            copies_ref[n, :, here] = excess
    return evolve * (jnp.exp(-state) - jnp.sqrt(squares))


def first_kernel(place_ref, own_ref, other_ref, a_ref, b_ref, drift_ref, copies_ref):
    stress, state, plate = start_of(own_ref, other_ref)
    drift_ref[...] = rates(stress, state, plate, half_of(place_ref, a_ref), half_of(place_ref, b_ref), copies_ref)


def stress_kernel(stage, place_ref, grid_ref, near_ref, near_other_ref, *refs):
    pieces, out_ref = refs[:4], refs[4]
    groups, members, dofs = grid_ref.shape
    group, core, bit = place_ref[GROUP], place_ref[CORE], place_ref[BIT]
    block_row = lax.broadcasted_iota(jnp.int32, (members, B), 1) // 32

    total = jnp.zeros((4 * members, dofs), jnp.float32)
    for dx in range(4):
        columns = []
        for dy in range(4):
            source = ((place_ref[YL] - dy) & 3) * 4 + ((place_ref[X] - dx) & 3)
            product = lax.dot_general(grid_ref[source], pieces[dx][dy, 0], NT, preferred_element_type=jnp.float32)
            rows = [jnp.where(block_row == i, product, 0.0).astype(jnp.bfloat16) for i in range(4)]
            columns.append(jnp.concatenate(rows, axis=0))
        factors = jnp.concatenate([pieces[dx][dy, 1] for dy in range(4)], axis=0)
        total = total + jnp.dot(jnp.concatenate(columns, axis=1), factors, preferred_element_type=jnp.float32)

    blocks = [total[i * members : (i + 1) * members] for i in range(4)]
    for i in range(2):
        blocks[i] = blocks[i] + lax.dot_general(grid_ref[group], near_ref[i], NT, preferred_element_type=jnp.float32)
    beside = group + 1 - core - bit
    edge = grid_ref[jnp.clip(beside, 0, groups - 1)]
    edge = jnp.where((beside >= 0) & (beside < groups), edge, jnp.zeros_like(edge))
    edge = lax.dot_general(edge, near_other_ref[...], NT, preferred_element_type=jnp.float32)
    for i in range(2):
        blocks[2 + i] = blocks[2 + i] + jnp.where(bit == 1 - i, edge, 0.0)

    for i, block in enumerate(blocks):
        high, low = (core if i < 2 else 1 - core), i % 2
        if stage < 3:
            out_ref[2 * high + low] = block
        else:
            out_ref[2 * high + bit, low] = block[: members // 2]
            out_ref[2 * high + 1 - bit, low] = block[members // 2 :]


def update_kernel(stage, place_ref, sums_ref, own_ref, other_ref, a_ref, b_ref, *refs):
    bit = place_ref[BIT]
    stress_start, state_start, plate = start_of(own_ref, other_ref)
    same = sums_ref[bit] + sums_ref[2 + bit]
    swap = sums_ref[1 - bit] + sums_ref[3 - bit]
    half = same.shape[0] // 2
    rate = -(same + jnp.concatenate([swap[half:], swap[:half]], axis=0))
    direct, evolve = half_of(place_ref, a_ref), half_of(place_ref, b_ref)
    if stage == 1:
        drift_ref, stress_out, state_out, drift_out, copies_ref = refs
        stress = stress_start + HSTEP * rate
        state = state_start + HSTEP * drift_ref[...]
        stress_out[...] = stress
        state_out[...] = state
        drift_out[...] = rates(stress, state, plate, direct, evolve, copies_ref)
    else:
        stress_ref, state_ref, drift_ref, mine_ref, send_ref, copies_ref = refs
        stress = 0.75 * stress_start + 0.25 * (stress_ref[...] + HSTEP * rate)
        state = 0.75 * state_start + 0.25 * (state_ref[...] + HSTEP * drift_ref[...])
        state = state + HSTEP * rates(stress, state, plate, direct, evolve, copies_ref)
        for ref, rows in ((mine_ref, slice(0, half)), (send_ref, slice(half, 2 * half))):
            ref[:, : 2 * B] = stress[rows]
            ref[:, 2 * B :] = state[rows]


def last_kernel(place_ref, sums_ref, mine_ref, other_ref, stress_ref, state_ref, stress_out, state_out):
    for n in range(2):
        middle = jnp.where(place_ref[BIT] == n, mine_ref[...], other_ref[...])
        rate = -(sums_ref[0, n] + sums_ref[1, n] + sums_ref[2, n] + sums_ref[3, n])
        here = slice(n * 2 * B, (n + 1) * 2 * B)
        stress_out[:, here] = stress_ref[:, here] / 3.0 + 2.0 / 3.0 * (middle[:, : 2 * B] + HSTEP * rate)
        here = slice(n * B, (n + 1) * B)
        state_out[:, here] = state_ref[:, here] / 3.0 + 2.0 / 3.0 * middle[:, 2 * B :]


def call(kernel, outs, operands, flops=0, scalars=1):
    outs = [jax.ShapeDtypeStruct(shape, dtype) for *shape, dtype in outs]
    bytes_accessed = sum(x.size * x.dtype.itemsize for x in [*operands, *outs])
    return pl.pallas_call(
        kernel,
        out_shape=outs,
        in_specs=[SMEM if n < scalars else VMEM for n in range(len(operands))],
        out_specs=[VMEM] * len(outs),
        compiler_params=pltpu.CompilerParams(vmem_limit_bytes=16 << 20),
        cost_estimate=pl.CostEstimate(flops=flops, bytes_accessed=bytes_accessed, transcendentals=0),
    )(*operands)


def local(stress, state, load_rate, a_param, b_param, near_band, u_far, v_far, ranks):
    bit, core, x_at = lax.axis_index("yb"), lax.axis_index("c"), lax.axis_index("x")
    y_at = lax.axis_index("ya") * 2 + bit
    group = lax.axis_index("yh") * 8 + lax.axis_index("z")
    place = jnp.stack([y_at, x_at, group, core, bit, group * 2 + core, y_at * 4 + x_at]).astype(jnp.int32)
    params = (a_param.reshape(1, -1), b_param.reshape(1, -1))
    members, dofs = stress.shape[0], 2 * B
    f32, bf16 = jnp.float32, jnp.bfloat16
    swap = ring(2, 1)

    keep, send, near = call(
        split_kernel,
        [(1, dofs, dofs, bf16), (2, dofs, dofs, bf16), (2, dofs, dofs, bf16)],
        (place, ranks, v_far, u_far, near_band),
        scalars=2,
    )
    own, away = call(pack_kernel, [(members, 5 * B, f32)] * 2, (place, stress, state, load_rate))
    got = lax.ppermute(send, "c", swap)
    other = lax.ppermute(away, "yb", swap)
    parts = (2, 2, dofs // 4, dofs)
    both = jnp.concatenate([keep[0].reshape(parts), got[0].reshape(parts)], axis=2)
    same, flip = both[0], both[1]
    along_y = [same] + [lax.ppermute(flip if k % 2 else same, ("ya", "yb"), ring(4, k)) for k in range(1, 4)]
    along_y = jnp.stack(along_y)
    pieces = [along_y] + [lax.ppermute(along_y, "x", ring(4, k)) for k in range(1, 4)]

    copies_shape = (16, 2 * members, dofs, bf16)
    whole, part = (2 * members, dofs, f32), (2 * members, B, f32)
    flops = 2 * 16 * (32 * 256 * 128 + 128 * 128 * 256)

    def partials(stage, copies):
        grid = lax.all_to_all(copies, ("yh", "z"), 0, 0)
        shape = (4, 2 * members, dofs, f32) if stage < 3 else (4, 2, members, dofs, f32)
        (sums,) = call(functools.partial(stress_kernel, stage), [shape], (place, grid, near, got[1], *pieces), flops)
        return lax.all_to_all(sums, ("c", "yb"), 0, 0)

    def update(stage, sums, outs, now):
        return call(functools.partial(update_kernel, stage), outs, (place, sums, own, other, *params, *now))

    drift, copies = call(first_kernel, [part, copies_shape], (place, own, other, *params))
    *now, copies = update(1, partials(1, copies), [whole, part, part, copies_shape], (drift,))
    packed = (members, 3 * B, f32)
    mine, away, copies = update(2, partials(2, copies), [packed, packed, copies_shape], now)
    theirs = lax.ppermute(away, "yb", swap)
    sums = partials(3, copies)
    outs = [(members, 2 * dofs, f32), (members, dofs, f32)]
    return call(last_kernel, outs, (place, sums, mine, theirs, stress, state))


def solution(mesh):
    fine = Mesh(mesh.devices.reshape(2, 8, 2, 2, 2, 4), ("yh", "z", "c", "ya", "yb", "x"))
    row, col = ("yh", "z", "c"), ("ya", "yb", "x")
    return jax.shard_map(
        local,
        mesh=fine,
        in_specs=(
            P(col, row),
            P(col, row),
            P(col, row),
            P(row),
            P(row),
            P(row, None),
            P(row, col, None, None),
            P(row, col, None, None),
            P(row, col),
        ),
        out_specs=(P(col, row), P(col, row)),
        check_vma=False,
    )
```

```python
import functools

import jax
import jax.numpy as jnp
from jax import lax
from jax.experimental import pallas as pl
from jax.experimental.pallas import tpu as pltpu
from jax.sharding import Mesh, PartitionSpec as P


B = 128
HSTEP = 0.2
RATE_UNIT = 1.0 / 1024.0

VMEM = pl.BlockSpec(memory_space=pltpu.VMEM)
SMEM = pl.BlockSpec(memory_space=pltpu.SMEM)
NT = (((1,), (1,)), ((), ()))

YL, X, GROUP, CORE, BIT, ROW, COL = range(7)


def ring(size, step):
    return [(i, (i + step) % size) for i in range(size)]


def prologue_kernel(place_ref, *refs):
    inputs, refs = refs[:9], refs[9:]
    own_ref, away_ref, params_ref, keep_ref, send_ref, near_out_ref = refs[:6]
    held, sems = refs[6:15], refs[15]
    copies = [pltpu.make_async_copy(inputs[n], held[n], sems.at[n]) for n in range(9)]
    for copy in copies:
        copy.start()
    for copy in copies:
        copy.wait()
    ranks_ref, stress_ref, state_ref, load_ref, a_ref, b_ref, near_ref, u_ref, v_ref = held
    core, bit = place_ref[CORE], place_ref[BIT]

    def halves(value):
        low, high = value[:, : value.shape[1] // 2], value[:, value.shape[1] // 2 :]
        return jnp.where(bit == 0, low, high), jnp.where(bit == 0, high, low)

    plate = load_ref[...].astype(jnp.float32) * RATE_UNIT
    for value, at in ((stress_ref[...], 0), (state_ref[...], 2 * B), (plate, 3 * B)):
        mine, other = halves(value)
        own_ref[:, at : at + mine.shape[1]] = mine
        away_ref[:, at : at + mine.shape[1]] = other
    params_ref[0:1, :] = halves(a_ref[...])[0]
    params_ref[1:2, :] = halves(b_ref[...])[0]

    block_rows, block_cols, slots, dofs = v_ref.shape
    slot = lax.broadcasted_iota(jnp.int32, (slots, dofs), 0)
    for flip in range(2):
        low = bit if flip == 0 else 1 - bit
        for i in range(block_rows):
            for out_ref, high in ((keep_ref.at[0], core), (send_ref.at[0], 1 - core)):
                j = 2 * high + low
                apart = jnp.abs(place_ref[ROW] * block_rows + i - place_ref[COL] * block_cols - j) >= 2
                rank = jnp.where(apart, ranks_ref[i, j], 0)
                at = (flip * 2 * block_rows + i) * slots
                out_ref[at : at + slots, :] = jnp.where(slot < rank, v_ref[i, j], 0).astype(v_ref.dtype)
                at = at + block_rows * slots
                out_ref[at : at + slots, :] = u_ref[i, j]
    first, second = slice(0, dofs), slice(dofs, 2 * dofs)
    tiles = [slice(s * dofs, (s + 1) * dofs) for s in range(3)]
    near_out_ref[0] = jnp.where(bit == 0, near_ref[first, tiles[1]], near_ref[first, tiles[2]])
    near_out_ref[1] = jnp.where(bit == 0, near_ref[second, tiles[0]], near_ref[second, tiles[1]])
    send_ref[1] = jnp.where(bit == 0, near_ref[second, tiles[2]], near_ref[first, tiles[0]])


def start_of(own_ref, other_ref):
    both = jnp.concatenate([own_ref[...], other_ref[...]], axis=0)
    return both[:, : 2 * B], both[:, 2 * B : 3 * B], both[:, 3 * B :]


def rates(stress, state, plate, direct, evolve, copies_ref):
    squares = 0.0
    for s in range(2):
        here = slice(s * B, (s + 1) * B)
        drive = stress[:, here] / direct
        rate = jnp.exp(drive - state) - jnp.exp(-drive - state)
        squares = squares + rate * rate
        excess = (rate - plate[:, here]).astype(jnp.bfloat16)
        for n in range(copies_ref.shape[0]):
            copies_ref[n, :, here] = excess
    return evolve * (jnp.exp(-state) - jnp.sqrt(squares))


def first_kernel(own_ref, other_ref, params_ref, drift_ref, copies_ref):
    stress, state, plate = start_of(own_ref, other_ref)
    drift_ref[...] = rates(stress, state, plate, params_ref[0:1, :], params_ref[1:2, :], copies_ref)


def stress_kernel(stage, place_ref, grid_ref, near_ref, near_other_ref, *refs):
    pieces, refs = refs[:4], refs[4:]
    out_ref = refs[-1]
    groups, members, dofs = grid_ref.shape
    group, core, bit = place_ref[GROUP], place_ref[CORE], place_ref[BIT]
    block_row = lax.broadcasted_iota(jnp.int32, (members, B), 1) // 32

    total = jnp.zeros((4 * members, dofs), jnp.float32)
    for dx in range(4):
        columns = []
        for dy in range(4):
            source = ((place_ref[YL] - dy) & 3) * 4 + ((place_ref[X] - dx) & 3)
            product = lax.dot_general(grid_ref[source], pieces[dx][dy, 0], NT, preferred_element_type=jnp.float32)
            rows = [jnp.where(block_row == i, product, 0.0).astype(jnp.bfloat16) for i in range(4)]
            columns.append(jnp.concatenate(rows, axis=0))
        factors = jnp.concatenate([pieces[dx][dy, 1] for dy in range(4)], axis=0)
        total = total + jnp.dot(jnp.concatenate(columns, axis=1), factors, preferred_element_type=jnp.float32)

    blocks = [total[i * members : (i + 1) * members] for i in range(4)]
    for i in range(2):
        blocks[i] = blocks[i] + lax.dot_general(grid_ref[group], near_ref[i], NT, preferred_element_type=jnp.float32)
    beside = group + 1 - core - bit
    edge = grid_ref[jnp.clip(beside, 0, groups - 1)]
    edge = jnp.where((beside >= 0) & (beside < groups), edge, jnp.zeros_like(edge))
    edge = lax.dot_general(edge, near_other_ref[...], NT, preferred_element_type=jnp.float32)
    for i in range(2):
        blocks[2 + i] = blocks[2 + i] + jnp.where(bit == 1 - i, edge, 0.0)

    for i, block in enumerate(blocks):
        high, low = (core if i < 2 else 1 - core), i % 2
        if stage < 3:
            out_ref[2 * high + low] = block
        else:
            here = slice(low * dofs, (low + 1) * dofs)
            out_ref[2 * high + bit, :, here] = block[: members // 2]
            out_ref[2 * high + 1 - bit, :, here] = block[members // 2 :]
    if stage == 3:
        for n in range(4):
            out_ref[n, :, 2 * dofs :] = refs[0][...]


def update_kernel(stage, place_ref, sums_ref, own_ref, other_ref, params_ref, *refs):
    bit = place_ref[BIT]
    stress_start, state_start, plate = start_of(own_ref, other_ref)
    same = sums_ref[bit] + sums_ref[2 + bit]
    swap = sums_ref[1 - bit] + sums_ref[3 - bit]
    half = same.shape[0] // 2
    rate = -(same + jnp.concatenate([swap[half:], swap[:half]], axis=0))
    direct, evolve = params_ref[0:1, :], params_ref[1:2, :]
    if stage == 1:
        drift_ref, stress_out, state_out, drift_out, copies_ref = refs
        stress = stress_start + HSTEP * rate
        state = state_start + HSTEP * drift_ref[...]
        stress_out[...] = stress
        state_out[...] = state
        drift_out[...] = rates(stress, state, plate, direct, evolve, copies_ref)
    else:
        stress_ref, state_ref, drift_ref, mine_ref, send_ref, copies_ref = refs
        stress = 0.75 * stress_start + 0.25 * (stress_ref[...] + HSTEP * rate)
        state = 0.75 * state_start + 0.25 * (state_ref[...] + HSTEP * drift_ref[...])
        state = state + HSTEP * rates(stress, state, plate, direct, evolve, copies_ref)
        for ref, rows in ((mine_ref, slice(0, half)), (send_ref, slice(half, 2 * half))):
            ref[:, : 2 * B] = stress[rows]
            ref[:, 2 * B :] = state[rows]


def last_kernel(place_ref, sums_ref, mine_ref, stress_ref, state_ref, stress_out, state_out):
    bit, dofs = place_ref[BIT], 2 * B
    theirs = sums_ref[2 * place_ref[CORE] + 1 - bit, :, 2 * dofs :]
    for n in range(2):
        middle = jnp.where(bit == n, mine_ref[...], theirs)
        here = slice(n * dofs, (n + 1) * dofs)
        rate = -(sums_ref[0, :, here] + sums_ref[1, :, here] + sums_ref[2, :, here] + sums_ref[3, :, here])
        stress_out[:, here] = stress_ref[:, here] / 3.0 + 2.0 / 3.0 * (middle[:, :dofs] + HSTEP * rate)
        here = slice(n * B, (n + 1) * B)
        state_out[:, here] = state_ref[:, here] / 3.0 + 2.0 / 3.0 * middle[:, dofs:]


def call(kernel, outs, operands, flops=0, scalars=0, whole=False):
    outs = [jax.ShapeDtypeStruct(shape, dtype) for *shape, dtype in outs]
    bytes_accessed = sum(x.size * x.dtype.itemsize for x in [*operands, *outs])
    place = pl.BlockSpec(memory_space=pltpu.HBM) if whole else VMEM
    scratch = [(pltpu.SMEM if x.size < 64 else pltpu.VMEM)(x.shape, x.dtype) for x in operands[scalars:]] if whole else []
    if whole:
        operands = [x if n < scalars else pltpu.with_memory_space_constraint(x, pltpu.HBM) for n, x in enumerate(operands)]
    return pl.pallas_call(
        kernel,
        out_shape=outs,
        in_specs=[SMEM if n < scalars else place for n in range(len(operands))],
        out_specs=[VMEM] * len(outs),
        scratch_shapes=scratch + [pltpu.SemaphoreType.DMA((len(scratch),))] if whole else [],
        compiler_params=pltpu.CompilerParams(vmem_limit_bytes=16 << 20),
        cost_estimate=pl.CostEstimate(flops=flops, bytes_accessed=bytes_accessed, transcendentals=0),
    )(*operands)


def local(stress, state, load_rate, a_param, b_param, near_band, u_far, v_far, ranks):
    bit, core, x_at = lax.axis_index("yb"), lax.axis_index("c"), lax.axis_index("x")
    y_at = lax.axis_index("ya") * 2 + bit
    group = lax.axis_index("yh") * 8 + lax.axis_index("z")
    place = jnp.stack([y_at, x_at, group, core, bit, group * 2 + core, y_at * 4 + x_at]).astype(jnp.int32)
    members, dofs = stress.shape[0], 2 * B
    f32, bf16 = jnp.float32, jnp.bfloat16
    swap = ring(2, 1)

    own, away, params, keep, send, near = call(
        prologue_kernel,
        [(members, 5 * B, f32)] * 2 + [(2, B, f32), (1, dofs, dofs, bf16), (2, dofs, dofs, bf16), (2, dofs, dofs, bf16)],
        (place, ranks, stress, state, load_rate, a_param.reshape(1, -1), b_param.reshape(1, -1), near_band, u_far, v_far),
        scalars=1,
        whole=True,
    )

    other = lax.ppermute(away, "yb", swap)
    got = lax.ppermute(send, "c", swap)
    parts = (2, 2, dofs // 4, dofs)
    both = jnp.concatenate([keep[0].reshape(parts), got[0].reshape(parts)], axis=2)
    same, flip = both[0], both[1]
    along_y = [lax.ppermute(flip if k % 2 else same, ("ya", "yb"), ring(4, k)) for k in range(1, 4)]
    along_y = jnp.stack([same] + along_y)
    pieces = [along_y] + [lax.ppermute(along_y, "x", ring(4, k)) for k in range(1, 4)]

    copies_shape = (16, 2 * members, dofs, bf16)
    whole, part = (2 * members, dofs, f32), (2 * members, B, f32)
    flops = 2 * 16 * (32 * 256 * 128 + 128 * 128 * 256)

    def partials(stage, copies, *more):
        grid = lax.all_to_all(copies, ("yh", "z"), 0, 0)
        shape = (4, *whole) if stage < 3 else (4, members, 7 * B, f32)
        operands = (place, grid, near, got[1], *pieces, *more)
        (sums,) = call(functools.partial(stress_kernel, stage), [shape], operands, flops, scalars=1)
        return lax.all_to_all(sums, ("c", "yb"), 0, 0)

    def update(stage, sums, outs, now):
        return call(functools.partial(update_kernel, stage), outs, (place, sums, own, other, params, *now), scalars=1)

    drift, copies = call(first_kernel, [part, copies_shape], (own, other, params))
    *now, copies = update(1, partials(1, copies), [whole, part, part, copies_shape], (drift,))
    packed = (members, 3 * B, f32)
    mine, away, copies = update(2, partials(2, copies), [packed, packed, copies_shape], now)
    outs = [(members, 2 * dofs, f32), (members, dofs, f32)]
    return call(last_kernel, outs, (place, partials(3, copies, away), mine, stress, state), scalars=1)


def solution(mesh):
    fine = Mesh(mesh.devices.reshape(2, 8, 2, 2, 2, 4), ("yh", "z", "c", "ya", "yb", "x"))
    row, col = ("yh", "z", "c"), ("ya", "yb", "x")
    return jax.shard_map(
        local,
        mesh=fine,
        in_specs=(
            P(col, row),
            P(col, row),
            P(col, row),
            P(row),
            P(row),
            P(row, None),
            P(row, col, None, None),
            P(row, col, None, None),
            P(row, col),
        ),
        out_specs=(P(col, row), P(col, row)),
        check_vma=False,
    )
```

```python
import functools

import jax
import jax.numpy as jnp
from jax import lax
from jax.experimental import pallas as pl
from jax.experimental.pallas import tpu as pltpu
from jax.sharding import Mesh, PartitionSpec as P


B = 128
HSTEP = 0.2
RATE_UNIT = 1.0 / 1024.0

VMEM = pl.BlockSpec(memory_space=pltpu.VMEM)
NT = (((1,), (1,)), ((), ()))

YL, X, GROUP, CORE, BIT, ROW, COL = range(7)


def ring(size, step):
    return [(i, (i + step) % size) for i in range(size)]


def place():
    bit, core = lax.axis_index("yb"), lax.axis_index("c")
    y_at, x_at = lax.axis_index("ya") * 2 + bit, lax.axis_index("x")
    group = lax.axis_index("yh") * 8 + lax.axis_index("z")
    return y_at, x_at, group, core, bit, group * 2 + core, y_at * 4 + x_at


def prologue_kernel(*refs):
    at_place = place()
    (*inputs, near_ref), refs = refs[:9], refs[9:]
    own_ref, away_ref, params_ref, keep_ref, send_ref, near_out_ref = refs[:6]
    held, sems = refs[6:14], refs[14]
    core, bit = at_place[CORE], at_place[BIT]
    copies = [pltpu.make_async_copy(inputs[n], held[n], sems.at[n]) for n in range(8)]
    size = near_out_ref.shape[1]
    tiles = ((0, 1 + bit, near_out_ref.at[0]), (1, bit, near_out_ref.at[1]), (1 - bit, 2 - 2 * bit, send_ref.at[1]))
    for n, (i, j, out_ref) in enumerate(tiles):
        at = [pl.ds(pl.multiple_of(k * size, size), size) for k in (i, j)]
        copies.append(pltpu.make_async_copy(near_ref.at[at[0], at[1]], out_ref, sems.at[8 + n]))
    for copy in copies:
        copy.start()
    for copy in copies[:8]:
        copy.wait()
    ranks_ref, stress_ref, state_ref, load_ref, a_ref, b_ref, u_ref, v_ref = held

    def halves(value):
        low, high = value[:, : value.shape[1] // 2], value[:, value.shape[1] // 2 :]
        return jnp.where(bit == 0, low, high), jnp.where(bit == 0, high, low)

    plate = load_ref[...].astype(jnp.float32) * RATE_UNIT
    for value, at in ((stress_ref[...], 0), (state_ref[...], 2 * B), (plate, 3 * B)):
        mine, other = halves(value)
        own_ref[:, at : at + mine.shape[1]] = mine
        away_ref[:, at : at + mine.shape[1]] = other
    params_ref[0:1, :] = halves(a_ref[...])[0]
    params_ref[1:2, :] = halves(b_ref[...])[0]
    params_ref[2:3, :] = jnp.full((1, B), bit, jnp.int32).astype(jnp.float32)

    block_rows, block_cols, slots, dofs = v_ref.shape
    slot = lax.broadcasted_iota(jnp.int32, (slots, dofs), 0)
    for flip in range(2):
        low = bit if flip == 0 else 1 - bit
        for i in range(block_rows):
            for out_ref, high in ((keep_ref.at[0], core), (send_ref.at[0], 1 - core)):
                j = 2 * high + low
                apart = jnp.abs(at_place[ROW] * block_rows + i - at_place[COL] * block_cols - j) >= 2
                rank = jnp.where(apart, ranks_ref[i, j], 0)
                at = (flip * 2 * block_rows + i) * slots
                out_ref[at : at + slots, :] = jnp.where(slot < rank, v_ref[i, j], 0).astype(v_ref.dtype)
                at = at + block_rows * slots
                out_ref[at : at + slots, :] = u_ref[i, j]
    for copy in copies[8:]:
        copy.wait()


def start_of(own_ref, other_ref):
    both = jnp.concatenate([own_ref[...], other_ref[...]], axis=0)
    return both[:, : 2 * B], both[:, 2 * B : 3 * B], both[:, 3 * B :]


def rates(stress, state, plate, direct, evolve, copies_ref):
    squares = 0.0
    for s in range(2):
        here = slice(s * B, (s + 1) * B)
        drive = stress[:, here] / direct
        rate = jnp.exp(drive - state) - jnp.exp(-drive - state)
        squares = squares + rate * rate
        excess = (rate - plate[:, here]).astype(jnp.bfloat16)
        for n in range(copies_ref.shape[0]):
            copies_ref[n, :, here] = excess
    return evolve * (jnp.exp(-state) - jnp.sqrt(squares))


def first_kernel(own_ref, other_ref, params_ref, drift_ref, copies_ref):
    stress, state, plate = start_of(own_ref, other_ref)
    drift_ref[...] = rates(stress, state, plate, params_ref[0:1, :], params_ref[1:2, :], copies_ref)


def stress_kernel(stage, grid_ref, near_ref, near_other_ref, *refs):
    at_place = place()
    pieces, refs = refs[:4], refs[4:]
    out_ref = refs[-1]
    groups, members, dofs = grid_ref.shape
    group, core, bit = at_place[GROUP], at_place[CORE], at_place[BIT]
    block_row = lax.broadcasted_iota(jnp.int32, (members, B), 1) // 32

    total = jnp.zeros((4 * members, dofs), jnp.float32)
    for dx in range(4):
        columns = []
        for dy in range(4):
            source = ((at_place[YL] - dy) & 3) * 4 + ((at_place[X] - dx) & 3)
            product = lax.dot_general(grid_ref[source], pieces[dx][dy, 0], NT, preferred_element_type=jnp.float32)
            rows = [jnp.where(block_row == i, product, 0.0).astype(jnp.bfloat16) for i in range(4)]
            columns.append(jnp.concatenate(rows, axis=0))
        factors = jnp.concatenate([pieces[dx][dy, 1] for dy in range(4)], axis=0)
        total = total + jnp.dot(jnp.concatenate(columns, axis=1), factors, preferred_element_type=jnp.float32)

    blocks = [total[i * members : (i + 1) * members] for i in range(4)]
    for i in range(2):
        blocks[i] = blocks[i] + lax.dot_general(grid_ref[group], near_ref[i], NT, preferred_element_type=jnp.float32)
    beside = group + 1 - core - bit
    edge = grid_ref[jnp.clip(beside, 0, groups - 1)]
    edge = jnp.where((beside >= 0) & (beside < groups), edge, jnp.zeros_like(edge))
    edge = lax.dot_general(edge, near_other_ref[...], NT, preferred_element_type=jnp.float32)
    for i in range(2):
        blocks[2 + i] = blocks[2 + i] + jnp.where(bit == 1 - i, edge, 0.0)

    for i, block in enumerate(blocks):
        high, low = (core if i < 2 else 1 - core), i % 2
        if stage < 3:
            swapped = jnp.concatenate([block[members // 2 :], block[: members // 2]], axis=0)
            out_ref[2 * high + low] = jnp.where(low == bit, block, swapped).astype(out_ref.dtype)
        else:
            here = slice(low * dofs, (low + 1) * dofs)
            out_ref[2 * high + bit, :, here] = block[: members // 2]
            out_ref[2 * high + 1 - bit, :, here] = block[members // 2 :]
    if stage == 3:
        for n in range(4):
            out_ref[n, :, 2 * dofs :] = jnp.where(n == 2 * core + 1 - bit, refs[0][...], 0.0)


def total_of(sums_ref, here=slice(None)):
    first, *rest = [sums_ref[n, :, here].astype(jnp.float32) for n in range(4)]
    return sum(rest, first)


def update_kernel(stage, sums_ref, own_ref, other_ref, params_ref, *refs):
    stress_start, state_start, plate = start_of(own_ref, other_ref)
    rate = -total_of(sums_ref)
    half = rate.shape[0] // 2
    direct, evolve = params_ref[0:1, :], params_ref[1:2, :]
    if stage == 1:
        drift_ref, stress_out, state_out, drift_out, copies_ref = refs
        stress = stress_start + HSTEP * rate
        state = state_start + HSTEP * drift_ref[...]
        stress_out[...] = stress
        state_out[...] = state
        drift_out[...] = rates(stress, state, plate, direct, evolve, copies_ref)
    else:
        stress_ref, state_ref, drift_ref, mine_ref, send_ref, copies_ref = refs
        stress = 0.75 * stress_start + 0.25 * (stress_ref[...] + HSTEP * rate)
        state = 0.75 * state_start + 0.25 * (state_ref[...] + HSTEP * drift_ref[...])
        state = state + HSTEP * rates(stress, state, plate, direct, evolve, copies_ref)
        for ref, rows in ((mine_ref, slice(0, half)), (send_ref, slice(half, 2 * half))):
            ref[:, : 2 * B] = stress[rows]
            ref[:, 2 * B :] = state[rows]


def last_kernel(sums_ref, mine_ref, params_ref, stress_ref, state_ref, stress_out, state_out):
    dofs, width = 2 * B, mine_ref.shape[1]
    low = jnp.broadcast_to(params_ref[2:3, :], (mine_ref.shape[0], B)) < 0.5
    low = jnp.concatenate([low] * (width // B), axis=1)
    mine, theirs = mine_ref[...], total_of(sums_ref, slice(2 * dofs, 2 * dofs + width))
    for n, middle in enumerate((jnp.where(low, mine, theirs), jnp.where(low, theirs, mine))):
        here = slice(n * dofs, (n + 1) * dofs)
        rate = -total_of(sums_ref, here)
        stress_out[:, here] = stress_ref[:, here] / 3.0 + 2.0 / 3.0 * (middle[:, :dofs] + HSTEP * rate)
        here = slice(n * B, (n + 1) * B)
        state_out[:, here] = state_ref[:, here] / 3.0 + 2.0 / 3.0 * middle[:, dofs:]


def call(kernel, outs, operands, flops=0, whole=False):
    outs = [jax.ShapeDtypeStruct(shape, dtype) for *shape, dtype in outs]
    bytes_accessed = sum(x.size * x.dtype.itemsize for x in [*operands, *outs])
    space = pl.BlockSpec(memory_space=pltpu.HBM) if whole else VMEM
    scratch = [(pltpu.SMEM if x.size < 64 else pltpu.VMEM)(x.shape, x.dtype) for x in operands[:-1]] if whole else []
    if whole:
        operands = [pltpu.with_memory_space_constraint(x, pltpu.HBM) for x in operands]
    return pl.pallas_call(
        kernel,
        out_shape=outs,
        in_specs=[space] * len(operands),
        out_specs=[VMEM] * len(outs),
        scratch_shapes=scratch + [pltpu.SemaphoreType.DMA((len(scratch) + 3,))] if whole else [],
        compiler_params=pltpu.CompilerParams(vmem_limit_bytes=16 << 20),
        cost_estimate=pl.CostEstimate(flops=flops, bytes_accessed=bytes_accessed, transcendentals=0),
    )(*operands)


def local(stress, state, load_rate, a_param, b_param, near_band, u_far, v_far, ranks):
    members, dofs = stress.shape[0], 2 * B
    f32, bf16 = jnp.float32, jnp.bfloat16
    swap = ring(2, 1)

    own, away, params, keep, send, near = call(
        prologue_kernel,
        [(members, 5 * B, f32)] * 2 + [(3, B, f32), (1, dofs, dofs, bf16), (2, dofs, dofs, bf16), (2, dofs, dofs, bf16)],
        (ranks, stress, state, load_rate, a_param.reshape(1, -1), b_param.reshape(1, -1), u_far, v_far, near_band),
        whole=True,
    )

    other = lax.ppermute(away, "yb", swap)
    got = lax.ppermute(send, "c", swap)
    parts = (2, 2, dofs // 4, dofs)
    both = jnp.concatenate([keep[0].reshape(parts), got[0].reshape(parts)], axis=2)
    same, flip = both[0], both[1]
    along_y = [lax.ppermute(flip if k % 2 else same, ("ya", "yb"), ring(4, k)) for k in range(1, 4)]
    along_y = jnp.stack([same] + along_y)
    pieces = [along_y] + [lax.ppermute(along_y, "x", ring(4, k)) for k in range(1, 4)]

    copies_shape = (16, 2 * members, dofs, bf16)
    whole, part = (2 * members, dofs, f32), (2 * members, B, f32)
    flops = 2 * 16 * (32 * 256 * 128 + 128 * 128 * 256)

    def partials(stage, copies, *more):
        grid = lax.all_to_all(copies, ("yh", "z"), 0, 0)
        shape = (4, 2 * members, dofs, f32) if stage < 3 else (4, members, 7 * B, f32)
        operands = (grid, near, got[1], *pieces, *more)
        (sums,) = call(functools.partial(stress_kernel, stage), [shape], operands, flops)
        return lax.all_to_all(sums, ("c", "yb"), 0, 0)

    def update(stage, sums, outs, now):
        return call(functools.partial(update_kernel, stage), outs, (sums, own, other, params, *now))

    drift, copies = call(first_kernel, [part, copies_shape], (own, other, params))
    *now, copies = update(1, partials(1, copies), [whole, part, part, copies_shape], (drift,))
    packed = (members, 3 * B, f32)
    mine, away, copies = update(2, partials(2, copies), [packed, packed, copies_shape], now)
    outs = [(members, 2 * dofs, f32), (members, dofs, f32)]
    return call(last_kernel, outs, (partials(3, copies, away), mine, params, stress, state))


def solution(mesh):
    fine = Mesh(mesh.devices.reshape(2, 8, 2, 2, 2, 4), ("yh", "z", "c", "ya", "yb", "x"))
    row, col = ("yh", "z", "c"), ("ya", "yb", "x")
    return jax.shard_map(
        local,
        mesh=fine,
        in_specs=(
            P(col, row),
            P(col, row),
            P(col, row),
            P(row),
            P(row),
            P(row, None),
            P(row, col, None, None),
            P(row, col, None, None),
            P(row, col),
        ),
        out_specs=(P(col, row), P(col, row)),
        check_vma=False,
    )
```
